256 devices in a mesh: frame: 8 (over z_hi, core), rank: 32 (over x, y, z_lo).
Axes of the slice: x: 4, y: 4, z: 8 (z_hi: 4, z_lo: 2; z = z_hi * 2 + z_lo), core: 2. Of those that a mesh axis runs over, the one named last changes fastest.
Arguments:
- layers: float32 [8, 32, 4, 32, 16384], P('frame', 'rank')
- depth_order: int32 [8, 32], P('frame'), may hold values from 0 to 31, as said below
- tile_slots: int32 [32], replicated, may hold values from 0 to 31, each once
Outputs:
- filtered: float32 [32, 8, 4, 16384], P('frame', None, None, 'rank')
- coverage: float32 [8], P('frame')
The draws below stay inside these ranges and needn't reach their ends.
Inputs may be any that keep to these rules, and one draw needn't show every extreme that they name: `depth_order`: each row is a permutation of the ranks in which, for every bit b, the ranks that agree on all bits from b upward take consecutive depths. `tile_slots`: slot s belongs to frame group s // 4.
All inputs are finite; a program needn't handle non-finite values.
Results may differ from the reference program's by a relative error of at most 0.00002.
Values sent between devices are 32-bit elements; how exact they have to be, the bound alone decides.
A program may use at most 64 MiB of HBM per device.

```python
import jax
import jax.numpy as jnp
from jax import lax

TILE = 128
TILES = 32
FRAMES = 8
RANKS = 32


def draw_layers(key, part):
    key_alpha, key_color, key_block = jax.random.split(jax.random.fold_in(key, 11), 3)
    piece_len = TILE * TILE // RANKS
    shape = (FRAMES, RANKS, 1, TILES, RANKS, piece_len)
    alpha = jnp.exp(jax.random.uniform(key_alpha, shape, jnp.float32, jnp.log(0.005), jnp.log(0.08)))
    position = jnp.arange(RANKS, dtype=jnp.float32) / max(RANKS - 1, 1)
    jitter = jax.random.uniform(key_block, (FRAMES, RANKS), jnp.float32, -0.35, 0.35)
    factor = jnp.minimum(jnp.exp(jnp.log(0.12) * (1.0 - position)[None, :] + jitter), 1.0)
    alpha = alpha * factor[:, None, None, None, :, None]
    alpha = alpha.reshape(FRAMES, RANKS, 1, TILES, TILE * TILE)
    color = alpha * jax.random.uniform(key_color, (FRAMES, RANKS, 3, TILES, TILE * TILE), jnp.float32)
    return jnp.concatenate([color, alpha], axis=2).astype(jnp.float32)


def draw_depth_order(key, part):
    levels = RANKS.bit_length() - 1
    ranks = jnp.arange(RANKS, dtype=jnp.int32)
    flips = jax.random.randint(jax.random.fold_in(key, 23), (FRAMES, max(levels, 1), RANKS), 0, 2).astype(jnp.int32)
    place = jnp.broadcast_to(ranks[None, :], (FRAMES, RANKS))
    for level in range(levels):
        parent = ranks >> level + 1
        place = place ^ flips[:, level, parent] << level
    frame_ids = jnp.arange(FRAMES, dtype=jnp.int32)[:, None]
    order = jnp.zeros((FRAMES, RANKS), jnp.int32).at[frame_ids, place].set(jnp.broadcast_to(ranks[None, :], (FRAMES, RANKS)))
    return order


def setup_inputs(seed: int = 0) -> dict:
    key_list = jax.random.split(jax.random.key(seed), 4)
    layers = draw_layers(jax.random.fold_in(key_list[3], 71), 0)
    depth_order = draw_depth_order(jax.random.fold_in(key_list[3], 71), 0)
    tile_slots = jax.random.permutation(key_list[2], TILES).astype(jnp.int32)
    return dict(layers=layers, depth_order=depth_order, tile_slots=tile_slots)


def one_frame(operands):
    frame_layers, order = operands

    def blend(total, rank_id):
        layer = lax.dynamic_index_in_dim(frame_layers, rank_id, 0, keepdims=False)
        return total + (1.0 - total[3:4]) * layer, None

    start = jnp.zeros(frame_layers.shape[1:], jnp.float32)
    total, unused = lax.scan(blend, start, order)
    return total


def reference(layers, depth_order, tile_slots):
    composite = lax.map(one_frame, (layers, depth_order))
    coverage = jnp.sum(composite[:, 3], axis=(1, 2)) / (TILES * TILE * TILE)
    picked = composite[:, :, tile_slots, :]
    before = jnp.concatenate([picked[:1], picked[:-1]], axis=0)
    after = jnp.concatenate([picked[1:], picked[-1:]], axis=0)
    smooth = 0.25 * before + 0.5 * picked + 0.25 * after
    filtered = jnp.transpose(smooth, (2, 0, 1, 3))
    return filtered, coverage
```

```python
import functools

import jax
import jax.numpy as jnp
from jax import lax
from jax.experimental import pallas as pl
from jax.experimental.pallas import tpu as pltpu
from jax.sharding import PartitionSpec as P

MESH = pl.DeviceIdType.MESH
LANES = 128
ROWS = 8
AHEAD = 2

CHUNKS = (
    ("alpha", 2, 0), ("alpha", 2, 1), ("swap", 0, 0),
    ("alpha", 2, 2), ("alpha", 2, 3), ("swap", 0, 2),
    ("alpha", 3, 0), ("alpha", 3, 1), ("swap", 1, 0),
    ("alpha", 3, 2), ("alpha", 3, 3), ("swap", 1, 2),
)


def blend(a, b, b_near):
    weight_a = 1.0 - b_near * b[:, 3:4]
    weight_b = 1.0 - (1.0 - b_near) * a[:, 3:4]
    return weight_a * a + weight_b * b


def blend4(values, flags):
    low = blend(values[0], values[1], flags[0])
    high = blend(values[2], values[3], flags[1])
    return blend(low, high, flags[2])


def kernel(
    layers, order, slots, out, cov,
    keep, half, alpha, ysend, ybuf, xsend, xbuf, vsend, vrecv, comp, chosen, picked, fbuf, csend, cbuf,
    keep_sem, zs, zr, ys, yr, xs, xr, vs, vr, fs, fr, cs, cr,
):
    rank = lax.axis_index("rank")
    frame = lax.axis_index("frame")
    x, y, z = lax.div(rank, 8), lax.rem(lax.div(rank, 2), 4), lax.rem(rank, 2)
    frames = fbuf.shape[1]
    pixels = layers.shape[1] * layers.shape[2]

    def at(px, py, pz):
        return {"rank": px * 8 + py * 2 + pz}

    partner = at(x, y, 1 - z)

    barrier = pltpu.get_barrier_semaphore()

    def greet(device):
        pl.semaphore_signal(barrier, inc=1, device_id=device, device_id_type=MESH)

    greet(partner)
    for d in range(1, 4):
        greet(at(x, lax.rem(y + d, 4), z))
        greet(at(lax.rem(x + d, 4), y, z))
    for d in range(1, frames):
        greet({"frame": lax.rem(frame + d, frames)})

    def tiles(group):
        return pl.ds(group * ROWS, ROWS)

    def rows_of(group):
        return slice(group * ROWS, (group + 1) * ROWS)

    def lanes(px, py, pz, tile):
        start = ((px * 8 + py * 2 + pz) * 4 + tile) * LANES
        return pl.ds(pl.multiple_of(start, LANES), LANES)

    kinds = [kind for kind, _, _ in CHUNKS]
    number = [kinds[:i].count(kind) for i, kind in enumerate(kinds)]

    def load_own(c):
        kind, tile, group = CHUNKS[c]

        def body(q, carry):
            py, px = lax.div(q, 4), lax.rem(q, 4)
            for u in range(2):
                if kind == "swap":
                    source = layers.at[:, tiles(group + u), lanes(px, py, z, tile)]
                else:
                    source = layers.at[:, tiles(group), lanes(px, py, u, tile)]
                pltpu.make_async_copy(source, keep.at[c, q, u], keep_sem.at[c]).start()
            return carry

        lax.fori_loop(0, 16, body, 0)

    def send_z(c):
        kind, tile, group = CHUNKS[c]
        n = number[c]

        def body(q, carry):
            py, px = lax.div(q, 4), lax.rem(q, 4)
            for u in range(2):
                if kind == "swap":
                    source = layers.at[:, tiles(group + u), lanes(px, py, 1 - z, tile)]
                    target = half.at[n, q, u]
                else:
                    source = layers.at[3, tiles(group), lanes(px, py, u, tile)]
                    target = alpha.at[n, q, u]
                remote(source, target, zs.at[c], zr.at[c], partner).start()
            return carry

        lax.fori_loop(0, 16, body, 0)

    def remote(src, dst, send_sem, recv_sem, device):
        return pltpu.make_async_remote_copy(
            src_ref=src, dst_ref=dst, send_sem=send_sem, recv_sem=recv_sem, device_id=device, device_id_type=MESH
        )

    def z_copy(c):
        box = half.at[number[c]] if kinds[c] == "swap" else alpha.at[number[c]]
        return remote(box, box, zs.at[c], zr.at[c], partner)

    def y_copy(c, d):
        return remote(ysend.at[c, d - 1], ybuf.at[c, d], ys.at[c, d - 1], yr.at[c, d - 1], at(x, lax.rem(y + d, 4), z))

    def x_copy(c, d):
        return remote(xsend.at[c, d - 1], xbuf.at[c, d], xs.at[c, d - 1], xr.at[c, d - 1], at(lax.rem(x + d, 4), y, z))

    def v_copy(c):
        n = number[c]
        return remote(vsend.at[n], vrecv.at[n], vs.at[n], vr.at[n], partner)

    def f_copy(tile, d):
        return remote(
            picked.at[tile, d], fbuf.at[tile, d], fs.at[tile, d - 1], fr.at[tile, d - 1],
            {"frame": lax.rem(frame + d, frames)},
        )

    def c_copy(phase, d):
        device = (at(lax.rem(x + d, 4), y, z), at(x, lax.rem(y + d, 4), z), partner)[phase]
        return remote(
            csend.at[phase], cbuf.at[phase, d - 1], cs.at[phase, d - 1], cr.at[phase, d - 1], device
        )

    for c in range(AHEAD):
        load_own(c)

    own_pair = (at(x, y, 0)["rank"], at(x, y, 1)["rank"])
    wanted = own_pair + tuple(at(x, k, 0)["rank"] for k in range(4)) + tuple(at(k, 0, 0)["rank"] for k in range(4))

    def find(k, found):
        here = order[k]
        return tuple(jnp.where(here == who, k, depth) for who, depth in zip(wanted, found))

    depth = lax.fori_loop(0, 32, find, (jnp.int32(0),) * len(wanted))

    def nearer(first, second):
        return jnp.where(depth[second] < depth[first], jnp.float32(1), jnp.float32(0))

    second_near = nearer(0, 1)
    partner_near = jnp.where(z == 0, second_near, 1.0 - second_near)
    y_flags = (nearer(2, 3), nearer(4, 5), nearer(2, 4))
    x_flags = (nearer(6, 7), nearer(8, 9), nearer(6, 8))

    row = lax.broadcasted_iota(jnp.int32, chosen.shape, 0)
    column = lax.broadcasted_iota(jnp.int32, chosen.shape, 1)
    wanted_tile = jnp.zeros(chosen.shape, jnp.int32)
    for d in range(frames):
        for j in range(4):
            wanted_tile = jnp.where(row // 4 == d * 4 + j, slots[lax.rem(frame + d, frames) * 4 + j], wanted_tile)
    hit = column == row % 4 * comp.shape[2] + wanted_tile
    chosen[...] = jnp.where(hit, jnp.float32(1), jnp.float32(0))

    pl.semaphore_wait(barrier, 1 + 6 + frames - 1)
    for c in range(AHEAD):
        send_z(c)

    def pair(c):
        kind = kinds[c]
        n = number[c]
        pltpu.make_async_copy(keep.at[c], keep.at[c], keep_sem.at[c]).wait()
        z_copy(c).wait_recv()

        def value(q):
            own = keep[c, q]
            if kind == "swap":
                return blend(own, half[n, q], partner_near)
            other = alpha[n, q]
            weight = 1.0 - partner_near * other
            opacity = weight * own[:, 3] + (1.0 - (1.0 - partner_near) * own[:, 3]) * other
            return jnp.concatenate([weight[:, None] * own[:, :3], opacity[:, None]], axis=1)

        for d in (2, 1, 3, 0):
            py = lax.rem(y + d, 4)

            def body(px, carry, d=d, py=py):
                result = value(py * 4 + px)
                if d == 0:
                    ybuf[c, 0, px] = result
                else:
                    ysend[c, d - 1, px] = result
                return carry

            lax.fori_loop(0, 4, body, 0)
            if d:
                y_copy(c, d).start()

    def over_y(c):
        for d in range(1, 4):
            y_copy(c, d).wait_recv()
        for d in (2, 1, 3, 0):
            px = lax.rem(x + d, 4)
            result = blend4([ybuf[c, lax.rem(y - k + 4, 4), px] for k in range(4)], y_flags)
            if d == 0:
                xbuf[c, 0] = result
            else:
                xsend[c, d - 1] = result
                x_copy(c, d).start()

    def over_x(c):
        kind, tile, group = CHUNKS[c]
        for d in range(1, 4):
            x_copy(c, d).wait_recv()
        result = blend4([xbuf[c, lax.rem(x - k + 4, 4)] for k in range(4)], x_flags)
        low, high = result[0], result[1]
        if kind == "swap":
            comp[tile, :, rows_of(group)] = low
            comp[tile, :, rows_of(group + 1)] = high
            csend[0] += low[3] + high[3]
        else:
            n = number[c]
            mine = jnp.where(z == 0, low, high)
            vsend[n] = jnp.where(z == 0, high, low)[:3]
            v_copy(c).start()
            comp[tile, :, rows_of(group)] = mine
            csend[0] += mine[3]

    def add_z(c):
        kind, tile, group = CHUNKS[c]
        v_copy(c).wait_recv()
        comp[tile, :3, rows_of(group)] += vrecv[number[c]]

    def send_frames(tile):
        picked[tile] = jnp.dot(
            chosen[...],
            comp[tile].reshape(4 * comp.shape[2], LANES),
            preferred_element_type=jnp.float32,
            precision=lax.Precision.HIGHEST,
        ).reshape(picked.shape[1:])
        for d in range(1, frames):
            f_copy(tile, d).start()
        fbuf[tile, 0] = picked[tile, 0]

    def smooth(tile):
        for d in range(1, frames):
            f_copy(tile, d).wait_recv()
        values = [fbuf[tile, lax.rem(frame - k + frames, frames)] for k in range(frames)]
        for k in range(frames):
            before, after = values[max(k - 1, 0)], values[min(k + 1, frames - 1)]
            result = 0.25 * before + 0.5 * values[k] + 0.25 * after
            for j in range(4):
                out[j, k, :, tile * LANES : (tile + 1) * LANES] = result[j * 4 : (j + 1) * 4]

    csend[0] = jnp.zeros((ROWS, LANES), jnp.float32)
    count = len(CHUNKS)
    left = [sum(tile == t for _, tile, _ in CHUNKS) for t in range(4)]
    sent = []

    def finished(c):
        tile = CHUNKS[c][1]
        left[tile] -= 1
        if left[tile] == 0:
            send_frames(tile)
            sent.append(tile)

    for step in range(count + 3):
        if step < count:
            if step + AHEAD < count:
                load_own(step + AHEAD)
                send_z(step + AHEAD)
            pair(step)
        if 0 <= step - 1 < count:
            over_y(step - 1)
        if 0 <= step - 2 < count:
            over_x(step - 2)
            if kinds[step - 2] == "swap":
                finished(step - 2)
        if 0 <= step - 3 < count and kinds[step - 3] == "alpha":
            add_z(step - 3)
            finished(step - 3)

    for phase, peers in enumerate((3, 3, 1)):
        for d in range(1, peers + 1):
            c_copy(phase, d).start()
        total = csend[phase]
        for d in range(1, peers + 1):
            c_copy(phase, d).wait_recv()
            total = total + cbuf[phase, d - 1]
        csend[phase + 1] = total
    cov[0] = jnp.sum(csend[3]) / pixels

    for t in sent:
        smooth(t)

    for c in range(count):
        z_copy(c).wait_send()
        for d in range(1, 4):
            y_copy(c, d).wait_send()
            x_copy(c, d).wait_send()
        if kinds[c] == "alpha":
            v_copy(c).wait_send()
    for t in sent:
        for d in range(1, frames):
            f_copy(t, d).wait_send()
    for phase, peers in enumerate((3, 3, 1)):
        for d in range(1, peers + 1):
            c_copy(phase, d).wait_send()


def shards(layers, depth_order, tile_slots):
    mine = layers[0, 0]
    frames = lax.axis_size("frame")
    count = len(CHUNKS)
    swaps = sum(kind == "swap" for kind, _, _ in CHUNKS)
    alphas = count - swaps
    block = (2, 4, ROWS, LANES)
    vmem = functools.partial(pltpu.VMEM, dtype=jnp.float32)
    dma = pltpu.SemaphoreType.DMA
    filtered, coverage = pl.pallas_call(
        kernel,
        out_shape=(
            jax.ShapeDtypeStruct((4, frames, 4, 4 * LANES), jnp.float32),
            jax.ShapeDtypeStruct((1,), jnp.float32),
        ),
        in_specs=[
            pl.BlockSpec(memory_space=pltpu.HBM),
            pl.BlockSpec(memory_space=pltpu.SMEM),
            pl.BlockSpec(memory_space=pltpu.SMEM),
        ],
        out_specs=(pl.BlockSpec(memory_space=pltpu.VMEM), pl.BlockSpec(memory_space=pltpu.SMEM)),
        scratch_shapes=[
            vmem((count, 16, *block)),
            vmem((swaps, 16, *block)),
            vmem((alphas, 16, 2, ROWS, LANES)),
            vmem((count, 3, 4, *block)),
            vmem((count, 4, 4, *block)),
            vmem((count, 3, *block)),
            vmem((count, 4, *block)),
            vmem((alphas, 3, ROWS, LANES)),
            vmem((alphas, 3, ROWS, LANES)),
            vmem((4, 4, 32, LANES)),
            vmem((16 * frames, 4 * 32)),
            vmem((4, frames, 16, LANES)),
            vmem((4, frames, 16, LANES)),
            vmem((4, ROWS, LANES)),
            vmem((3, 3, ROWS, LANES)),
            dma((count,)),
            dma((count,)),
            dma((count,)),
            dma((count, 3)),
            dma((count, 3)),
            dma((count, 3)),
            dma((count, 3)),
            dma((alphas,)),
            dma((alphas,)),
            dma((4, frames - 1)),
            dma((4, frames - 1)),
            dma((3, 3)),
            dma((3, 3)),
        ],
        compiler_params=pltpu.CompilerParams(
            collective_id=0, has_side_effects=True, vmem_limit_bytes=56 * 1024 * 1024
        ),
        name="composite",
    )(mine, depth_order[0], tile_slots)
    return (filtered, coverage)


def solution(mesh):
    placed = (P("frame", "rank", None, None, None), P("frame", None), P())
    return jax.shard_map(
        shards,
        mesh=mesh,
        in_specs=placed,
        out_specs=(P("frame", None, None, "rank"), P("frame")),
        check_vma=False,
    )
```

```python
import functools

import jax
import jax.numpy as jnp
from jax import lax
from jax.experimental import pallas as pl
from jax.experimental.pallas import tpu as pltpu
from jax.sharding import PartitionSpec as P

MESH = pl.DeviceIdType.MESH
LANES = 128
ROWS = 8

CHUNKS = (
    *(("alpha", tile, group) for tile in (2, 3) for group in range(4)),
    ("alpha", 0, 0),
    *(("swap", 0, group) for group in range(1, 4)),
    *(("swap", 1, group) for group in range(4)),
)
LAG_X, LAG_V = 3, 5
SUM_PEERS = (3, 3, 1)
UNITS = {"alpha": 2, "swap": 1}
SEND_Z = {"alpha": 2.9, "swap": 5.6}
SEND_Y = {"alpha": 5.9, "swap": 2.95}
LEAD = 0.0


def blend(a, b, b_near):
    weight_a = 1.0 - b_near * b[:, 3:4]
    weight_b = 1.0 - (1.0 - b_near) * a[:, 3:4]
    return weight_a * a + weight_b * b


def blend4(values, flags):
    low = blend(values[0], values[1], flags[0])
    high = blend(values[2], values[3], flags[1])
    return blend(low, high, flags[2])


def kernel(
    layers, order, slots, out, cov,
    keep_a, keep_s, half, alpha, ysend_a, ysend_s, ybuf_a, ybuf_s, xsend_a, xsend_s, xbuf_a, xbuf_s, vsend, vrecv, comp, chosen, picked, fbuf, csend, cbuf,
    keep_sem, zs, zr, ys, yr, xs, xr, vs, vr, fs, fr, cs, cr,
):
    rank = lax.axis_index("rank")
    frame = lax.axis_index("frame")
    x, y, z = lax.div(rank, 8), lax.rem(lax.div(rank, 2), 4), lax.rem(rank, 2)
    frames = fbuf.shape[1]
    keep = {"alpha": keep_a, "swap": keep_s}
    ysend = {"alpha": ysend_a, "swap": ysend_s}
    ybuf = {"alpha": ybuf_a, "swap": ybuf_s}
    xsend = {"alpha": xsend_a, "swap": xsend_s}
    xbuf = {"alpha": xbuf_a, "swap": xbuf_s}
    pixels = layers.shape[1] * layers.shape[2]

    def at(px, py, pz):
        return {"rank": px * 8 + py * 2 + pz}

    partner = at(x, y, 1 - z)

    barrier = pltpu.get_barrier_semaphore()

    def greet(device):
        pl.semaphore_signal(barrier, inc=1, device_id=device, device_id_type=MESH)

    for d in range(1, frames):
        greet({"frame": lax.rem(frame + d, frames)})
    for d in range(1, 4):
        greet(at(x, lax.rem(y + d, 4), z))
        greet(at(lax.rem(x + d, 4), y, z))
    greet(partner)

    def tiles(group):
        return pl.ds(group * ROWS, ROWS)

    def rows_of(group):
        return slice(group * ROWS, (group + 1) * ROWS)

    def lanes(px, py, pz, tile):
        start = ((px * 8 + py * 2 + pz) * 4 + tile) * LANES
        return pl.ds(pl.multiple_of(start, LANES), LANES)

    kinds = [kind for kind, _, _ in CHUNKS]
    number = [kinds[:i].count(kind) for i, kind in enumerate(kinds)]

    def load_own(c):
        kind, tile, group = CHUNKS[c]

        def body(q, carry):
            py, px = lax.div(q, 4), lax.rem(q, 4)
            for u in range(UNITS[kind]):
                if kind == "swap":
                    source = layers.at[:, tiles(group), lanes(px, py, z, tile)]
                else:
                    source = layers.at[:, tiles(group), lanes(px, py, u, tile)]
                pltpu.make_async_copy(source, keep[kind].at[number[c], q, u], keep_sem.at[c]).start()
            return carry

        lax.fori_loop(0, 16, body, 0)

    def send_z(c):
        kind, tile, group = CHUNKS[c]
        n = number[c]

        def body(q, carry):
            py, px = lax.div(q, 4), lax.rem(q, 4)
            for u in range(UNITS[kind]):
                if kind == "swap":
                    source = layers.at[:, tiles(group), lanes(px, py, 1 - z, tile)]
                    target = half.at[n, q, u]
                else:
                    source = layers.at[3, tiles(group), lanes(px, py, u, tile)]
                    target = alpha.at[n, q, u]
                remote(source, target, zs.at[c], zr.at[c], partner).start()
            return carry

        lax.fori_loop(0, 16, body, 0)

    def remote(src, dst, send_sem, recv_sem, device):
        return pltpu.make_async_remote_copy(
            src_ref=src, dst_ref=dst, send_sem=send_sem, recv_sem=recv_sem, device_id=device, device_id_type=MESH
        )

    def z_copy(c):
        box = half.at[number[c]] if kinds[c] == "swap" else alpha.at[number[c]]
        return remote(box, box, zs.at[c], zr.at[c], partner)

    def y_copy(c, d):
        kind, n = kinds[c], number[c]
        return remote(ysend[kind].at[n, d - 1], ybuf[kind].at[n, d], ys.at[c, d - 1], yr.at[c, d - 1], at(x, lax.rem(y + d, 4), z))

    def x_copy(c, d):
        kind, n = kinds[c], number[c]
        return remote(xsend[kind].at[n, d - 1], xbuf[kind].at[n, d], xs.at[c, d - 1], xr.at[c, d - 1], at(lax.rem(x + d, 4), y, z))

    def v_copy(c):
        n = number[c]
        return remote(vsend.at[n], vrecv.at[n], vs.at[n], vr.at[n], partner)

    def f_copy(tile, d):
        return remote(
            picked.at[tile, d], fbuf.at[tile, d], fs.at[tile, d - 1], fr.at[tile, d - 1],
            {"frame": lax.rem(frame + d, frames)},
        )

    def c_copy(phase, d):
        device = (at(lax.rem(x + d, 4), y, z), at(x, lax.rem(y + d, 4), z), partner)[phase]
        return remote(
            csend.at[phase], cbuf.at[phase, d - 1], cs.at[phase, d - 1], cr.at[phase, d - 1], device
        )

    load_own(0)
    load_own(1)

    own_pair = (at(x, y, 0)["rank"], at(x, y, 1)["rank"])
    wanted = own_pair + tuple(at(x, k, 0)["rank"] for k in range(4)) + tuple(at(k, 0, 0)["rank"] for k in range(4))

    def find(k, found):
        here = order[k]
        return tuple(jnp.where(here == who, k, depth) for who, depth in zip(wanted, found))

    depth = lax.fori_loop(0, 32, find, (jnp.int32(0),) * len(wanted))

    def nearer(first, second):
        return jnp.where(depth[second] < depth[first], jnp.float32(1), jnp.float32(0))

    second_near = nearer(0, 1)
    partner_near = jnp.where(z == 0, second_near, 1.0 - second_near)
    y_flags = (nearer(2, 3), nearer(4, 5), nearer(2, 4))
    x_flags = (nearer(6, 7), nearer(8, 9), nearer(6, 8))

    row = lax.broadcasted_iota(jnp.int32, chosen.shape, 0)
    column = lax.broadcasted_iota(jnp.int32, chosen.shape, 1)
    wanted_tile = jnp.zeros(chosen.shape, jnp.int32)
    for d in range(frames):
        for j in range(4):
            wanted_tile = jnp.where(row // 4 == d * 4 + j, slots[lax.rem(frame + d, frames) * 4 + j], wanted_tile)
    hit = column == row % 4 * comp.shape[2] + wanted_tile
    chosen[...] = jnp.where(hit, jnp.float32(1), jnp.float32(0))

    pl.semaphore_wait(barrier, 1 + 6 + frames - 1)
    send_z(0)
    send_z(1)

    def pair(c):
        kind = kinds[c]
        n = number[c]
        own_all = keep[kind].at[n]
        pltpu.make_async_copy(own_all, own_all, keep_sem.at[c]).wait()
        z_copy(c).wait_recv()

        def value(q):
            own = keep[kind][n, q]
            if kind == "swap":
                return blend(own, half[n, q], partner_near)
            other = alpha[n, q]
            weight = 1.0 - partner_near * other
            opacity = weight * own[:, 3] + (1.0 - (1.0 - partner_near) * own[:, 3]) * other
            return jnp.concatenate([weight[:, None] * own[:, :3], opacity[:, None]], axis=1)

        for d in (2, 1, 3, 0):
            py = lax.rem(y + d, 4)

            def body(px, carry, d=d, py=py):
                result = value(py * 4 + px)
                if d == 0:
                    ybuf[kind][n, 0, px] = result
                else:
                    ysend[kind][n, d - 1, px] = result
                return carry

            lax.fori_loop(0, 4, body, 0)
            if d:
                y_copy(c, d).start()

    def over_y(c):
        kind, n = kinds[c], number[c]
        for d in range(1, 4):
            y_copy(c, d).wait_recv()
        for d in (2, 1, 3, 0):
            px = lax.rem(x + d, 4)
            result = blend4([ybuf[kind][n, lax.rem(y - k + 4, 4), px] for k in range(4)], y_flags)
            if d == 0:
                xbuf[kind][n, 0] = result
            else:
                xsend[kind][n, d - 1] = result
                x_copy(c, d).start()

    def over_x(c):
        kind, tile, group = CHUNKS[c]
        for d in range(1, 4):
            x_copy(c, d).wait_recv()
        result = blend4([xbuf[kind][number[c], lax.rem(x - k + 4, 4)] for k in range(4)], x_flags)
        if kind == "swap":
            comp[tile, :, rows_of(group)] = result[0]
            csend[0] += result[0, 3]
        else:
            low, high = result[0], result[1]
            n = number[c]
            mine = jnp.where(z == 0, low, high)
            vsend[n] = jnp.where(z == 0, high, low)[:3]
            v_copy(c).start()
            comp[tile, :, rows_of(group)] = mine
            csend[0] += mine[3]

    def add_z(c):
        kind, tile, group = CHUNKS[c]
        v_copy(c).wait_recv()
        comp[tile, :3, rows_of(group)] += vrecv[number[c]]

    def send_frames(tile):
        picked[tile] = jnp.dot(
            chosen[...],
            comp[tile].reshape(4 * comp.shape[2], LANES),
            preferred_element_type=jnp.float32,
            precision=lax.Precision.HIGHEST,
        ).reshape(picked.shape[1:])
        for d in range(1, frames):
            f_copy(tile, d).start()
        fbuf[tile, 0] = picked[tile, 0]

    def smooth(tile):
        for d in range(1, frames):
            f_copy(tile, d).wait_recv()
        values = [fbuf[tile, lax.rem(frame - k + frames, frames)] for k in range(frames)]
        for k in range(frames):
            before, after = values[max(k - 1, 0)], values[min(k + 1, frames - 1)]
            result = 0.25 * before + 0.5 * values[k] + 0.25 * after
            for j in range(4):
                out[j, k, :, tile * LANES : (tile + 1) * LANES] = result[j * 4 : (j + 1) * 4]

    csend[0] = jnp.zeros((ROWS, LANES), jnp.float32)
    count = len(CHUNKS)
    left = [sum(tile == t for _, tile, _ in CHUNKS) for t in range(4)]
    sent = []

    def finished(c):
        tile = CHUNKS[c][1]
        left[tile] -= 1
        if left[tile] == 0:
            send_frames(tile)
            sent.append(tile)

    def start_sum(phase):
        for d in range(1, SUM_PEERS[phase] + 1):
            c_copy(phase, d).start()

    def end_sum(phase):
        total = csend[phase]
        for d in range(1, SUM_PEERS[phase] + 1):
            c_copy(phase, d).wait_recv()
            total = total + cbuf[phase, d - 1]
        csend[phase + 1] = total

    issued = 2
    z_time = SEND_Z[kinds[0]] + SEND_Z[kinds[1]]
    y_time = 0.0
    for step in range(count + LAG_V):
        if step < count:
            pair(step)
            y_time += SEND_Y[kinds[step]]
            while issued < count and (issued <= step + 1 or z_time < y_time + LEAD):
                load_own(issued)
                send_z(issued)
                z_time += SEND_Z[kinds[issued]]
                issued += 1
        if 0 <= step - 1 < count:
            over_y(step - 1)
        done = step - LAG_X
        if 0 <= done < count:
            over_x(done)
            if done == count - 1:
                start_sum(0)
            if kinds[done] == "swap":
                finished(done)
        done = step - LAG_V
        if 0 <= done < count and kinds[done] == "alpha":
            add_z(done)
            finished(done)

    for t in sent[:-1]:
        smooth(t)
    for phase in range(len(SUM_PEERS)):
        if phase:
            start_sum(phase)
        end_sum(phase)
    cov[0] = jnp.sum(csend[len(SUM_PEERS)]) / pixels
    smooth(sent[-1])

    for c in range(count):
        z_copy(c).wait_send()
        for d in range(1, 4):
            y_copy(c, d).wait_send()
            x_copy(c, d).wait_send()
        if kinds[c] == "alpha":
            v_copy(c).wait_send()
    for t in sent:
        for d in range(1, frames):
            f_copy(t, d).wait_send()
    for phase, peers in enumerate(SUM_PEERS):
        for d in range(1, peers + 1):
            c_copy(phase, d).wait_send()


def shards(layers, depth_order, tile_slots):
    mine = layers[0, 0]
    frames = lax.axis_size("frame")
    count = len(CHUNKS)
    swaps = sum(kind == "swap" for kind, _, _ in CHUNKS)
    alphas = count - swaps
    block = {"alpha": (2, 4, ROWS, LANES), "swap": (1, 4, ROWS, LANES)}
    vmem = functools.partial(pltpu.VMEM, dtype=jnp.float32)
    dma = pltpu.SemaphoreType.DMA
    filtered, coverage = pl.pallas_call(
        kernel,
        out_shape=(
            jax.ShapeDtypeStruct((4, frames, 4, 4 * LANES), jnp.float32),
            jax.ShapeDtypeStruct((1,), jnp.float32),
        ),
        in_specs=[
            pl.BlockSpec(memory_space=pltpu.HBM),
            pl.BlockSpec(memory_space=pltpu.SMEM),
            pl.BlockSpec(memory_space=pltpu.SMEM),
        ],
        out_specs=(pl.BlockSpec(memory_space=pltpu.VMEM), pl.BlockSpec(memory_space=pltpu.SMEM)),
        scratch_shapes=[
            vmem((alphas, 16, *block["alpha"])),
            vmem((swaps, 16, *block["swap"])),
            vmem((swaps, 16, *block["swap"])),
            vmem((alphas, 16, 2, ROWS, LANES)),
            vmem((alphas, 3, 4, *block["alpha"])),
            vmem((swaps, 3, 4, *block["swap"])),
            vmem((alphas, 4, 4, *block["alpha"])),
            vmem((swaps, 4, 4, *block["swap"])),
            vmem((alphas, 3, *block["alpha"])),
            vmem((swaps, 3, *block["swap"])),
            vmem((alphas, 4, *block["alpha"])),
            vmem((swaps, 4, *block["swap"])),
            vmem((alphas, 3, ROWS, LANES)),
            vmem((alphas, 3, ROWS, LANES)),
            vmem((4, 4, 32, LANES)),
            vmem((16 * frames, 4 * 32)),
            vmem((4, frames, 16, LANES)),
            vmem((4, frames, 16, LANES)),
            vmem((4, ROWS, LANES)),
            vmem((3, 3, ROWS, LANES)),
            dma((count,)),
            dma((count,)),
            dma((count,)),
            dma((count, 3)),
            dma((count, 3)),
            dma((count, 3)),
            dma((count, 3)),
            dma((alphas,)),
            dma((alphas,)),
            dma((4, frames - 1)),
            dma((4, frames - 1)),
            dma((3, 3)),
            dma((3, 3)),
        ],
        compiler_params=pltpu.CompilerParams(
            collective_id=0, has_side_effects=True, vmem_limit_bytes=56 * 1024 * 1024
        ),
        name="composite",
    )(mine, depth_order[0], tile_slots)
    return (filtered, coverage)


def solution(mesh):
    placed = (P("frame", "rank", None, None, None), P("frame", None), P())
    return jax.shard_map(
        shards,
        mesh=mesh,
        in_specs=placed,
        out_specs=(P("frame", None, None, "rank"), P("frame")),
        check_vma=False,
    )
```

```python
import functools

import jax
import jax.numpy as jnp
from jax import lax
from jax.experimental import pallas as pl
from jax.experimental.pallas import tpu as pltpu
from jax.sharding import PartitionSpec as P

MESH = pl.DeviceIdType.MESH
LANES = 128
ROWS = 8

CHUNKS = (
    *(("alpha", tile, group) for tile in (2, 3) for group in range(4)),
    ("alpha", 0, 0),
    *(("swap", 0, group) for group in range(1, 4)),
    *(("swap", 1, group) for group in range(4)),
)
LAG_X, LAG_V = 4, 6
SUM_PEERS = (3, 3, 1)
UNITS = {"alpha": 2, "swap": 1}
SEND_Z = {"alpha": 2.9, "swap": 5.6}
SEND_Y = {"alpha": 5.9, "swap": 2.95}
LEAD = 0.0


def blend(a, b, b_near):
    weight_a = 1.0 - b_near * b[:, 3:4]
    weight_b = 1.0 - (1.0 - b_near) * a[:, 3:4]
    return weight_a * a + weight_b * b


def blend4(values, flags):
    low = blend(values[0], values[1], flags[0])
    high = blend(values[2], values[3], flags[1])
    return blend(low, high, flags[2])


def kernel(
    layers, order, slots, out, cov,
    keep_a, keep_s, half, alpha, ysend_a, ysend_s, ybuf_a, ybuf_s, xsend_a, xsend_s, xbuf_a, xbuf_s, vsend, vrecv, comp, chosen, picked, fbuf, csend, cbuf,
    keep_sem, zs, zr, ys, yr, xs, xr, vs, vr, fs, fr, cs, cr,
):
    rank = lax.axis_index("rank")
    frame = lax.axis_index("frame")
    x, y, z = lax.div(rank, 8), lax.rem(lax.div(rank, 2), 4), lax.rem(rank, 2)
    frames = fbuf.shape[1]
    keep = {"alpha": keep_a, "swap": keep_s}
    ysend = {"alpha": ysend_a, "swap": ysend_s}
    ybuf = {"alpha": ybuf_a, "swap": ybuf_s}
    xsend = {"alpha": xsend_a, "swap": xsend_s}
    xbuf = {"alpha": xbuf_a, "swap": xbuf_s}
    pixels = layers.shape[1] * layers.shape[2]

    def at(px, py, pz):
        return {"rank": px * 8 + py * 2 + pz}

    partner = at(x, y, 1 - z)

    barrier = pltpu.get_barrier_semaphore()

    def greet(device):
        pl.semaphore_signal(barrier, inc=1, device_id=device, device_id_type=MESH)

    for d in range(1, frames):
        greet({"frame": lax.rem(frame + d, frames)})
    for d in range(1, 4):
        greet(at(x, lax.rem(y + d, 4), z))
        greet(at(lax.rem(x + d, 4), y, z))
    greet(partner)

    def tiles(group):
        return pl.ds(group * ROWS, ROWS)

    def rows_of(group):
        return slice(group * ROWS, (group + 1) * ROWS)

    def lanes(px, py, pz, tile):
        start = ((px * 8 + py * 2 + pz) * 4 + tile) * LANES
        return pl.ds(pl.multiple_of(start, LANES), LANES)

    kinds = [kind for kind, _, _ in CHUNKS]
    number = [kinds[:i].count(kind) for i, kind in enumerate(kinds)]

    def load_own(c):
        kind, tile, group = CHUNKS[c]

        def body(q, carry):
            py, px = lax.div(q, 4), lax.rem(q, 4)
            for u in range(UNITS[kind]):
                if kind == "swap":
                    source = layers.at[:, tiles(group), lanes(px, py, z, tile)]
                else:
                    source = layers.at[:, tiles(group), lanes(px, py, u, tile)]
                pltpu.make_async_copy(source, keep[kind].at[number[c], q, u], keep_sem.at[c]).start()
            return carry

        lax.fori_loop(0, 16, body, 0)

    def send_z(c):
        kind, tile, group = CHUNKS[c]
        n = number[c]

        def body(q, carry):
            py, px = lax.div(q, 4), lax.rem(q, 4)
            for u in range(UNITS[kind]):
                if kind == "swap":
                    source = layers.at[:, tiles(group), lanes(px, py, 1 - z, tile)]
                    target = half.at[n, q, u]
                else:
                    source = layers.at[3, tiles(group), lanes(px, py, u, tile)]
                    target = alpha.at[n, q, u]
                remote(source, target, zs.at[c], zr.at[c], partner).start()
            return carry

        lax.fori_loop(0, 16, body, 0)

    def remote(src, dst, send_sem, recv_sem, device):
        return pltpu.make_async_remote_copy(
            src_ref=src, dst_ref=dst, send_sem=send_sem, recv_sem=recv_sem, device_id=device, device_id_type=MESH
        )

    def z_copy(c):
        box = half.at[number[c]] if kinds[c] == "swap" else alpha.at[number[c]]
        return remote(box, box, zs.at[c], zr.at[c], partner)

    def y_copy(c, d):
        kind, n = kinds[c], number[c]
        return remote(ysend[kind].at[n, d - 1], ybuf[kind].at[n, d], ys.at[c, d - 1], yr.at[c, d - 1], at(x, lax.rem(y + d, 4), z))

    def x_copy(c, d):
        kind, n = kinds[c], number[c]
        return remote(xsend[kind].at[n, d - 1], xbuf[kind].at[n, d], xs.at[c, d - 1], xr.at[c, d - 1], at(lax.rem(x + d, 4), y, z))

    def v_copy(c):
        n = number[c]
        return remote(vsend.at[n], vrecv.at[n], vs.at[n], vr.at[n], partner)

    def f_copy(tile, d):
        return remote(
            picked.at[tile, d], fbuf.at[tile, d], fs.at[tile, d - 1], fr.at[tile, d - 1],
            {"frame": lax.rem(frame + d, frames)},
        )

    def c_copy(phase, d):
        device = (at(lax.rem(x + d, 4), y, z), at(x, lax.rem(y + d, 4), z), partner)[phase]
        return remote(
            csend.at[phase], cbuf.at[phase, d - 1], cs.at[phase, d - 1], cr.at[phase, d - 1], device
        )

    for c in range(16):
        load_own(c)

    own_pair = (at(x, y, 0)["rank"], at(x, y, 1)["rank"])
    wanted = own_pair + tuple(at(x, k, 0)["rank"] for k in range(4)) + tuple(at(k, 0, 0)["rank"] for k in range(4))

    def find(k, found):
        here = order[k]
        return tuple(jnp.where(here == who, k, depth) for who, depth in zip(wanted, found))

    depth = lax.fori_loop(0, 32, find, (jnp.int32(0),) * len(wanted))

    def nearer(first, second):
        return jnp.where(depth[second] < depth[first], jnp.float32(1), jnp.float32(0))

    second_near = nearer(0, 1)
    partner_near = jnp.where(z == 0, second_near, 1.0 - second_near)
    y_flags = (nearer(2, 3), nearer(4, 5), nearer(2, 4))
    x_flags = (nearer(6, 7), nearer(8, 9), nearer(6, 8))

    row = lax.broadcasted_iota(jnp.int32, chosen.shape, 0)
    column = lax.broadcasted_iota(jnp.int32, chosen.shape, 1)
    wanted_tile = jnp.zeros(chosen.shape, jnp.int32)
    for d in range(frames):
        for j in range(4):
            wanted_tile = jnp.where(row // 4 == d * 4 + j, slots[lax.rem(frame + d, frames) * 4 + j], wanted_tile)
    hit = column == row % 4 * comp.shape[2] + wanted_tile
    chosen[...] = jnp.where(hit, jnp.float32(1), jnp.float32(0))

    pl.semaphore_wait(barrier, 1 + 6 + frames - 1)
    send_z(0)
    send_z(1)

    def pair(c):
        kind = kinds[c]
        n = number[c]
        own_all = keep[kind].at[n]
        pltpu.make_async_copy(own_all, own_all, keep_sem.at[c]).wait()
        z_copy(c).wait_recv()

        def value(q):
            own = keep[kind][n, q]
            if kind == "swap":
                return blend(own, half[n, q], partner_near)
            other = alpha[n, q]
            weight = 1.0 - partner_near * other
            opacity = weight * own[:, 3] + (1.0 - (1.0 - partner_near) * own[:, 3]) * other
            return jnp.concatenate([weight[:, None] * own[:, :3], opacity[:, None]], axis=1)

        for d in (2, 1, 3, 0):
            py = lax.rem(y + d, 4)

            def body(px, carry, d=d, py=py):
                result = value(py * 4 + px)
                if d == 0:
                    ybuf[kind][n, 0, px] = result
                else:
                    ysend[kind][n, d - 1, px] = result
                return carry

            lax.fori_loop(0, 4, body, 0)
            if d:
                y_copy(c, d).start()

    def over_y(c):
        kind, n = kinds[c], number[c]
        for d in range(1, 4):
            y_copy(c, d).wait_recv()
        for d in (2, 1, 3, 0):
            px = lax.rem(x + d, 4)
            result = blend4([ybuf[kind][n, lax.rem(y - k + 4, 4), px] for k in range(4)], y_flags)
            if d == 0:
                xbuf[kind][n, 0] = result
            else:
                xsend[kind][n, d - 1] = result
                x_copy(c, d).start()

    def over_x(c):
        kind, tile, group = CHUNKS[c]
        for d in range(1, 4):
            x_copy(c, d).wait_recv()
        result = blend4([xbuf[kind][number[c], lax.rem(x - k + 4, 4)] for k in range(4)], x_flags)
        if kind == "swap":
            comp[tile, :, rows_of(group)] = result[0]
            csend[0] += result[0, 3]
        else:
            low, high = result[0], result[1]
            n = number[c]
            mine = jnp.where(z == 0, low, high)
            vsend[n] = jnp.where(z == 0, high, low)[:3]
            v_copy(c).start()
            comp[tile, :, rows_of(group)] = mine
            csend[0] += mine[3]

    def add_z(c):
        kind, tile, group = CHUNKS[c]
        v_copy(c).wait_recv()
        comp[tile, :3, rows_of(group)] += vrecv[number[c]]

    def send_frames(tile):
        picked[tile] = jnp.dot(
            chosen[...],
            comp[tile].reshape(4 * comp.shape[2], LANES),
            preferred_element_type=jnp.float32,
            precision=lax.Precision.HIGHEST,
        ).reshape(picked.shape[1:])
        for d in range(1, frames):
            f_copy(tile, d).start()
        fbuf[tile, 0] = picked[tile, 0]

    def smooth(tile):
        for d in range(1, frames):
            f_copy(tile, d).wait_recv()
        values = [fbuf[tile, lax.rem(frame - k + frames, frames)] for k in range(frames)]
        for k in range(frames):
            before, after = values[max(k - 1, 0)], values[min(k + 1, frames - 1)]
            result = 0.25 * before + 0.5 * values[k] + 0.25 * after
            for j in range(4):
                out[j, k, :, tile * LANES : (tile + 1) * LANES] = result[j * 4 : (j + 1) * 4]

    csend[0] = jnp.zeros((ROWS, LANES), jnp.float32)
    count = len(CHUNKS)
    left = [sum(tile == t for _, tile, _ in CHUNKS) for t in range(4)]
    sent = []

    def finished(c):
        tile = CHUNKS[c][1]
        left[tile] -= 1
        if left[tile] == 0:
            send_frames(tile)
            sent.append(tile)

    def start_sum(phase):
        for d in range(1, SUM_PEERS[phase] + 1):
            c_copy(phase, d).start()

    def end_sum(phase):
        total = csend[phase]
        for d in range(1, SUM_PEERS[phase] + 1):
            c_copy(phase, d).wait_recv()
            total = total + cbuf[phase, d - 1]
        csend[phase + 1] = total

    issued = 2
    z_time = SEND_Z[kinds[0]] + SEND_Z[kinds[1]]
    y_time = 0.0
    for step in range(count + LAG_V):
        if step < count:
            pair(step)
            y_time += SEND_Y[kinds[step]]
            while issued < count and (issued <= step + 1 or z_time < y_time + LEAD):
                send_z(issued)
                z_time += SEND_Z[kinds[issued]]
                issued += 1
        if 0 <= step - 1 < count:
            over_y(step - 1)
        done = step - LAG_X
        if 0 <= done < count:
            over_x(done)
            if done == count - 1:
                start_sum(0)
            if kinds[done] == "swap":
                finished(done)
        done = step - LAG_V
        if 0 <= done < count and kinds[done] == "alpha":
            add_z(done)
            finished(done)

    for t in sent[:-1]:
        smooth(t)
    for phase in range(len(SUM_PEERS)):
        if phase:
            start_sum(phase)
        end_sum(phase)
    cov[0] = jnp.sum(csend[len(SUM_PEERS)]) / pixels
    smooth(sent[-1])

    for c in range(count):
        z_copy(c).wait_send()
        for d in range(1, 4):
            y_copy(c, d).wait_send()
            x_copy(c, d).wait_send()
        if kinds[c] == "alpha":
            v_copy(c).wait_send()
    for t in sent:
        for d in range(1, frames):
            f_copy(t, d).wait_send()
    for phase, peers in enumerate(SUM_PEERS):
        for d in range(1, peers + 1):
            c_copy(phase, d).wait_send()


def shards(layers, depth_order, tile_slots):
    mine = layers[0, 0]
    frames = lax.axis_size("frame")
    count = len(CHUNKS)
    swaps = sum(kind == "swap" for kind, _, _ in CHUNKS)
    alphas = count - swaps
    block = {"alpha": (2, 4, ROWS, LANES), "swap": (1, 4, ROWS, LANES)}
    vmem = functools.partial(pltpu.VMEM, dtype=jnp.float32)
    dma = pltpu.SemaphoreType.DMA
    filtered, coverage = pl.pallas_call(
        kernel,
        out_shape=(
            jax.ShapeDtypeStruct((4, frames, 4, 4 * LANES), jnp.float32),
            jax.ShapeDtypeStruct((1,), jnp.float32),
        ),
        in_specs=[
            pl.BlockSpec(memory_space=pltpu.HBM),
            pl.BlockSpec(memory_space=pltpu.SMEM),
            pl.BlockSpec(memory_space=pltpu.SMEM),
        ],
        out_specs=(pl.BlockSpec(memory_space=pltpu.VMEM), pl.BlockSpec(memory_space=pltpu.SMEM)),
        scratch_shapes=[
            vmem((alphas, 16, *block["alpha"])),
            vmem((swaps, 16, *block["swap"])),
            vmem((swaps, 16, *block["swap"])),
            vmem((alphas, 16, 2, ROWS, LANES)),
            vmem((alphas, 3, 4, *block["alpha"])),
            vmem((swaps, 3, 4, *block["swap"])),
            vmem((alphas, 4, 4, *block["alpha"])),
            vmem((swaps, 4, 4, *block["swap"])),
            vmem((alphas, 3, *block["alpha"])),
            vmem((swaps, 3, *block["swap"])),
            vmem((alphas, 4, *block["alpha"])),
            vmem((swaps, 4, *block["swap"])),
            vmem((alphas, 3, ROWS, LANES)),
            vmem((alphas, 3, ROWS, LANES)),
            vmem((4, 4, 32, LANES)),
            vmem((16 * frames, 4 * 32)),
            vmem((4, frames, 16, LANES)),
            vmem((4, frames, 16, LANES)),
            vmem((4, ROWS, LANES)),
            vmem((3, 3, ROWS, LANES)),
            dma((count,)),
            dma((count,)),
            dma((count,)),
            dma((count, 3)),
            dma((count, 3)),
            dma((count, 3)),
            dma((count, 3)),
            dma((alphas,)),
            dma((alphas,)),
            dma((4, frames - 1)),
            dma((4, frames - 1)),
            dma((3, 3)),
            dma((3, 3)),
        ],
        compiler_params=pltpu.CompilerParams(
            collective_id=0, has_side_effects=True, vmem_limit_bytes=56 * 1024 * 1024
        ),
        name="composite",
    )(mine, depth_order[0], tile_slots)
    return (filtered, coverage)


def solution(mesh):
    placed = (P("frame", "rank", None, None, None), P("frame", None), P())
    return jax.shard_map(
        shards,
        mesh=mesh,
        in_specs=placed,
        out_specs=(P("frame", None, None, "rank"), P("frame")),
        check_vma=False,
    )
```
